32 devices in a mesh: fsdp: 8 (over y, x, core), dp: 4 (over z).
Axes of the slice: x: 2, y: 2, z: 4, core: 2. Of those that a mesh axis runs over, the one named last changes fastest.
Arguments:
- tokens: bfloat16 [32768, 768], P(('fsdp', 'dp')), may hold values from -6 to 6
- absorbed: int32 [32768], P(('fsdp', 'dp')), may hold values from 0 to 1, as said below
- noise_level: int32 [32], P(('fsdp', 'dp')), may hold values from 0 to 255
- cotangent: bfloat16 [32768, 768], P(('fsdp', 'dp')), may hold values from -6 to 6
- level_table: bfloat16 [256, 128], P('fsdp'), may hold values from -6 to 6
- absorb_vector: bfloat16 [768], P('fsdp'), may hold values from -6 to 6
- attn_gain: bfloat16 [768], P('fsdp'), may hold values from 0.5 to 1.5
- qkv_weight: bfloat16 [768, 2304], P('fsdp'), may hold values from -0.21875 to 0.21875
- out_weight: bfloat16 [768, 768], P('fsdp'), may hold values from -2 to 2
- mlp_gain: bfloat16 [768], P('fsdp'), may hold values from 0.5 to 1.5
- up_weight: bfloat16 [768, 3072], P('fsdp'), may hold values from -0.21875 to 0.21875
- up_bias: bfloat16 [3072], P('fsdp'), may hold values from -3 to 3
- down_weight: bfloat16 [3072, 768], P('fsdp'), may hold values from -0.109375 to 0.109375
- down_bias: bfloat16 [768], P('fsdp'), may hold values from -1.75 to 1.75
- mod_weight: bfloat16 [128, 4608], P('fsdp'), may hold values from -0.5 to 0.5
- mod_bias: bfloat16 [4608], P('fsdp'), may hold values from -3 to 3
Outputs:
- block_out: bfloat16 [32768, 768], P(('fsdp', 'dp'))
- tokens_grad: bfloat16 [32768, 768], P(('fsdp', 'dp'))
- level_table_grad: float32 [256, 128], P('fsdp')
- absorb_vector_grad: float32 [768], P('fsdp')
- attn_gain_grad: float32 [768], P('fsdp')
- qkv_weight_grad: float32 [768, 2304], P('fsdp')
- out_weight_grad: float32 [768, 768], P('fsdp')
- mlp_gain_grad: float32 [768], P('fsdp')
- up_weight_grad: float32 [768, 3072], P('fsdp')
- up_bias_grad: float32 [3072], P('fsdp')
- down_weight_grad: float32 [3072, 768], P('fsdp')
- down_bias_grad: float32 [768], P('fsdp')
- mod_weight_grad: float32 [128, 4608], P('fsdp')
- mod_bias_grad: float32 [4608], P('fsdp')
The draws below stay inside these ranges and needn't reach their ends.
Inputs may be any that keep to these rules, and one draw needn't show every extreme that they name: `absorbed`: within each sequence of 1024 tokens the ones form a few spans of uneven lengths.
All inputs are finite; a program needn't handle non-finite values.
Results may differ from the reference program's by a relative error of at most 0.017.
The reference program's roundings to bfloat16 on the way count: a program that leaves them out, or rounds other values in their place, can miss the bound.
Values may be sent and summed in bfloat16 or wider, within the bound.
No kernel may reach another device: no remote copies, remote signals or barrier semaphores. Data moves between devices by JAX's collectives and lax.ppermute only.
A program may use at most 256 MiB of HBM per device.

```python
import jax
import jax.numpy as jnp
from jax import lax

D = 768
HEADS = 12
HEAD = 64
FF = 3072
TEMB = 128
LEVELS = 256
LEN = 1024
SEQS = 32
TOKENS = 32768


def draw_absorbed(key, part):
    seq_count = TOKENS // LEN
    first_key, second_key = jax.random.split(jax.random.fold_in(key, 17))
    starts = jax.random.randint(first_key, (seq_count, 6), 0, LEN)
    spans = jax.random.randint(second_key, (seq_count, 6), 1, LEN // 6 + 2)
    positions = jnp.arange(LEN)[None, None, :]
    inside = (positions >= starts[:, :, None]) & (positions < starts[:, :, None] + spans[:, :, None])
    return jnp.any(inside, axis=1).astype(jnp.int32).reshape(TOKENS)


def place_ends(result, key, smallest, high):
    shape = result.shape
    spot = [jax.random.randint(jax.random.fold_in(key, axis), (), 0, shape[axis]) for axis in range(len(shape))]
    result = result.at[tuple(spot)].set(smallest)
    longest = shape.index(max(shape))
    spot[longest] = (spot[longest] + 1) % shape[longest]
    return result.at[tuple(spot)].set(high)


def levels(key, extent, cuts, low, top_value):
    level = 1.0
    for position, parts in cuts:
        steps = jax.random.uniform(jax.random.fold_in(jax.random.fold_in(key, 6), position), (parts,), jnp.float32, low / len(cuts), top_value / len(cuts))
        level = level * jnp.repeat(jnp.exp(steps), extent[position] // parts).reshape((-1,) + (1,) * (len(extent) - 1 - position))
    return level


def scatter_about(key, dims, deviation, most, cuts=(), kind=jnp.bfloat16):
    drawn = deviation * jax.random.normal(key, dims, jnp.float32)
    if cuts:
        drawn = drawn * levels(key, dims, cuts, -0.22, 0.18)
    return jnp.clip(drawn, -most, most).astype(kind)


def setup_inputs(seed: int = 0) -> dict:
    seeds = jax.random.split(jax.random.key(seed), 17)
    tokens = scatter_about(seeds[0], (TOKENS, D), 1.0, 6.0, ((0, 32),))
    absorbed = draw_absorbed(jax.random.fold_in(seeds[16], 71), 0)
    noise_level = place_ends(jax.random.randint(seeds[2], (SEQS,), 0, LEVELS), jax.random.fold_in(seeds[2], 1), 0, LEVELS - 1).astype(jnp.int32)
    cotangent = scatter_about(seeds[3], (TOKENS, D), 1.0, 6.0, ((0, 32),))
    level_table = scatter_about(seeds[4], (LEVELS, TEMB), 1.0, 6.0, ((0, 8),))
    absorb_vector = scatter_about(seeds[5], (D,), 1.0, 6.0, ((0, 8),))
    attn_gain = jnp.clip(1.0 + 0.1 * jax.random.normal(seeds[6], (D,), jnp.float32), 0.5, 1.5).astype(jnp.bfloat16)
    qkv_weight = scatter_about(seeds[7], (D, 3 * D), D ** -0.5, 0.21875, ((0, 8),))
    out_weight = scatter_about(seeds[8], (D, D), (D * 12 // LEN) ** -0.5, 2.0, ((0, 8),))
    mlp_gain = jnp.clip(1.0 + 0.1 * jax.random.normal(seeds[9], (D,), jnp.float32), 0.5, 1.5).astype(jnp.bfloat16)
    up_weight = scatter_about(seeds[10], (D, FF), D ** -0.5, 0.21875, ((0, 8),))
    up_bias = scatter_about(seeds[11], (FF,), 0.5, 3.0, ((0, 8),))
    down_weight = scatter_about(seeds[12], (FF, D), FF ** -0.5, 0.109375, ((0, 8),))
    down_bias = scatter_about(seeds[13], (D,), 0.3, 1.75, ((0, 8),))
    mod_weight = scatter_about(seeds[14], (TEMB, 6 * D), TEMB ** -0.5, 0.5, ((0, 8),))
    mod_bias = scatter_about(seeds[15], (6 * D,), 0.5, 3.0, ((0, 8),))
    return {"tokens": tokens, "absorbed": absorbed, "noise_level": noise_level, "cotangent": cotangent, "level_table": level_table, "absorb_vector": absorb_vector, "attn_gain": attn_gain, "qkv_weight": qkv_weight, "out_weight": out_weight, "mlp_gain": mlp_gain, "up_weight": up_weight, "up_bias": up_bias, "down_weight": down_weight, "down_bias": down_bias, "mod_weight": mod_weight, "mod_bias": mod_bias}


@jax.custom_vjp
def low(v):
    return lax.optimization_barrier(v.astype(jnp.bfloat16)).astype(jnp.float32)

@jax.custom_vjp
def low_back(v):
    return v

def low_keep(v):
    return (low(v), None)

def low_pass(kept, grad):
    return (grad,)

def back_keep(v):
    return (v, None)

def back_low(kept, grad):
    return (low(grad),)
low.defvjp(low_keep, low_pass)
low_back.defvjp(back_keep, back_low)
HIGHEST = lax.Precision.HIGHEST
EPSILON = 1e-05

def matmul(left, right):
    return jnp.dot(left, right, precision=HIGHEST)

def normalize(values):
    centred = values - lax.optimization_barrier(jnp.mean(values, axis=-1, keepdims=True))
    return centred * lax.rsqrt(lax.optimization_barrier(jnp.mean(centred * centred, axis=-1, keepdims=True)) + EPSILON)

def rotary(length, head_size):
    half_size = head_size // 2
    inverse = 10000.0 ** (-2.0 * jnp.arange(half_size, dtype=jnp.float32) / head_size)
    angles = jnp.arange(length, dtype=jnp.float32)[:, None] * inverse[None, :]
    angles = jnp.concatenate([angles, angles], axis=1)
    return (jnp.cos(angles)[:, None, :], jnp.sin(angles)[:, None, :])

def rotate(values, cosine, sine):
    half_size = values.shape[-1] // 2
    swapped = jnp.concatenate([-values[..., half_size:], values[..., :half_size]], axis=-1)
    return values * cosine + swapped * sine

def block(inputs, absorbed, level, weights):
    level_table, absorb_vector, attn_gain, qkv_weight, out_weight, mlp_gain, up_weight, up_bias, down_weight, down_bias, mod_weight, mod_bias = weights
    length = inputs.shape[0]
    condition = jax.nn.silu(level_table[level])
    modulation = low_back(matmul(low(condition)[None, :], mod_weight)[0] + mod_bias)
    shift_one, scale_one, gate_one, shift_two, scale_two, gate_two = jnp.split(modulation, 6)
    start_rows = jnp.where(absorbed[:, None] > 0, absorb_vector[None, :], inputs)
    hidden_one = low(normalize(start_rows) * attn_gain * (1.0 + scale_one) + shift_one)
    projected = low_back(matmul(hidden_one, qkv_weight)).reshape(length, 3, HEADS, HEAD)
    cosine, sine = rotary(length, HEAD)
    queries = low(rotate(projected[:, 0], cosine, sine))
    key_rows = low(rotate(projected[:, 1], cosine, sine))
    values = low(projected[:, 2])
    scores = low_back(jnp.einsum('qhd,khd->hqk', queries, key_rows, precision=HIGHEST) * HEAD ** (-0.5))
    probs_low = low(jax.nn.softmax(scores, axis=-1))
    mixed_rows = jnp.einsum('hqk,khd->qhd', probs_low, values, precision=HIGHEST).reshape(length, HEADS * HEAD)
    mixed_rows = low(low_back(mixed_rows))
    attended = low_back(matmul(mixed_rows, out_weight))
    middle = start_rows + gate_one * attended
    hidden_two = low(normalize(middle) * mlp_gain * (1.0 + scale_two) + shift_two)
    up_values = low_back(matmul(hidden_two, up_weight) + up_bias)
    activated = low(jax.nn.gelu(up_values, approximate=True))
    branch = low_back(matmul(activated, down_weight) + down_bias)
    return middle + gate_two * branch

def reference(tokens, absorbed, noise_level, cotangent, level_table, absorb_vector, attn_gain, qkv_weight, out_weight, mlp_gain, up_weight, up_bias, down_weight, down_bias, mod_weight, mod_bias):
    weights = tuple((member.astype(jnp.float32) for member in (level_table, absorb_vector, attn_gain, qkv_weight, out_weight, mlp_gain, up_weight, up_bias, down_weight, down_bias, mod_weight, mod_bias)))
    model_width = tokens.shape[1]
    seq_count = noise_level.shape[0]
    inputs = tokens.astype(jnp.float32).reshape(seq_count, -1, model_width)
    grads_in = cotangent.astype(jnp.float32).reshape(seq_count, -1, model_width)
    masks = absorbed.reshape(seq_count, -1)

    def one_sequence(totals, members):
        seq_tokens, seq_mask, seq_level, seq_grad = members
        outputs, pullback = jax.vjp(lambda given, params: block(given, seq_mask, seq_level, params), seq_tokens, weights)
        token_grad, weight_grads = pullback(seq_grad)
        totals = tuple((total_one + grad_one for total_one, grad_one in zip(totals, weight_grads)))
        return (totals, (outputs.astype(jnp.bfloat16), token_grad.astype(jnp.bfloat16)))
    zeros = tuple((jnp.zeros_like(member) for member in weights))
    totals, (outputs, token_grads) = lax.scan(one_sequence, zeros, (inputs, masks, noise_level, grads_in))
    return (outputs.reshape(-1, model_width), token_grads.reshape(-1, model_width), totals[0], totals[1], totals[2], totals[3], totals[4], totals[5], totals[6], totals[7], totals[8], totals[9], totals[10], totals[11])
```

```python
import jax
import jax.numpy as jnp
from jax import lax
from jax.sharding import PartitionSpec as P

HEAD = 64


EPSILON = 1e-05
ROOT_TERM = 0.7978845608028654
CUBIC_TERM = 0.044715


def product(left, right):
    return jnp.dot(left, right, preferred_element_type=jnp.float32)


def product_left(left, right):
    return lax.dot_general(
        left, right, (((0,), (0,)), ((), ())), preferred_element_type=jnp.float32
    )


def product_right(left, right):
    return lax.dot_general(
        left, right, (((1,), (1,)), ((), ())), preferred_element_type=jnp.float32
    )


def normalize(values):
    centred = values - jnp.mean(values, axis=-1, keepdims=True)
    inverse = lax.rsqrt(jnp.mean(centred * centred, axis=-1, keepdims=True) + EPSILON)
    return (centred * inverse, inverse)


def norm_back(grads, unit_rows, inverse):
    return inverse * (
        grads
        - jnp.mean(grads, axis=-1, keepdims=True)
        - unit_rows * jnp.mean(grads * unit_rows, axis=-1, keepdims=True)
    )


def rotary(length, head_size):
    half_size = head_size // 2
    inverse = 10000.0 ** (-2.0 * jnp.arange(half_size, dtype=jnp.float32) / head_size)
    angles = jnp.arange(length, dtype=jnp.float32)[:, None] * inverse[None, :]
    angles = jnp.concatenate([angles, angles], axis=1)
    return (jnp.cos(angles)[:, None, :], jnp.sin(angles)[:, None, :])


def swap_halves(values):
    half_size = values.shape[-1] // 2
    return jnp.concatenate([-values[..., half_size:], values[..., :half_size]], axis=-1)


def rotate(values, cosine, sine):
    return values * cosine + swap_halves(values) * sine


def rotate_back(grads, cosine, sine):
    return grads * cosine - swap_halves(grads * sine)


def gelu_slope(up_values):
    tanh_term = jnp.tanh(ROOT_TERM * (up_values + CUBIC_TERM * up_values * up_values * up_values))
    return 0.5 * (1.0 + tanh_term) + 0.5 * up_values * (1.0 - tanh_term * tanh_term) * ROOT_TERM * (
        1.0 + 3.0 * CUBIC_TERM * up_values * up_values
    )


def pair_forward(queries, key_rows, values):
    length = queries.shape[0]
    left = queries.reshape(length, 2, HEAD)
    right = key_rows.reshape(length, 2, HEAD)
    value_rows = values.reshape(length, 2, HEAD)
    scores = jnp.einsum("qhd,khd->hqk", left, right, preferred_element_type=jnp.float32) * HEAD ** (
        -0.5
    )
    highest = jnp.max(scores, axis=-1, keepdims=True)
    exponent = jnp.exp(scores - highest)
    totals = jnp.sum(exponent, axis=-1, keepdims=True)
    probs_low = (exponent / totals).astype(jnp.bfloat16)
    output = jnp.einsum("hqk,khd->qhd", probs_low, value_rows, preferred_element_type=jnp.float32)
    return (output.reshape(length, 2 * HEAD), (highest + jnp.log(totals))[:, :, 0])


def pair_backward(queries, key_rows, values, log_totals, grad_rows):
    length = queries.shape[0]
    left = queries.reshape(length, 2, HEAD)
    right = key_rows.reshape(length, 2, HEAD)
    value_rows = values.reshape(length, 2, HEAD)
    grad_heads = grad_rows.reshape(length, 2, HEAD)
    scores = jnp.einsum("qhd,khd->hqk", left, right, preferred_element_type=jnp.float32) * HEAD ** (
        -0.5
    )
    probs = jnp.exp(scores - log_totals[:, :, None])
    grad_probs = jnp.einsum(
        "qhd,khd->hqk", grad_heads, value_rows, preferred_element_type=jnp.float32
    )
    grad_values = jnp.einsum(
        "hqk,qhd->khd", probs.astype(jnp.bfloat16), grad_heads, preferred_element_type=jnp.float32
    )
    grad_scores = (
        probs * (grad_probs - jnp.sum(probs * grad_probs, axis=-1, keepdims=True))
    ).astype(jnp.bfloat16)
    grad_queries = jnp.einsum(
        "hqk,khd->qhd", grad_scores, right, preferred_element_type=jnp.float32
    ) * HEAD ** (-0.5)
    grad_keys = jnp.einsum(
        "hqk,qhd->khd", grad_scores, left, preferred_element_type=jnp.float32
    ) * HEAD ** (-0.5)
    return (
        grad_queries.reshape(length, 2 * HEAD),
        grad_keys.reshape(length, 2 * HEAD),
        grad_values.reshape(length, 2 * HEAD),
    )


def sequence_forward(members):
    queries, key_rows, values = members
    outputs = []
    log_parts = []
    for first in range(0, queries.shape[1], 2 * HEAD):
        output, log_totals = pair_forward(
            queries[:, first : first + 2 * HEAD],
            key_rows[:, first : first + 2 * HEAD],
            values[:, first : first + 2 * HEAD],
        )
        outputs.append(output)
        log_parts.append(log_totals)
    return (
        jnp.concatenate(outputs, axis=1).astype(jnp.bfloat16),
        jnp.concatenate(log_parts, axis=0),
    )


def sequence_backward(members):
    queries, key_rows, values, log_totals, grad_rows = members
    query_parts = []
    key_parts = []
    value_parts = []
    for first in range(0, queries.shape[1], 2 * HEAD):
        pair_index = first // HEAD
        grad_query, grad_key, grad_value = pair_backward(
            queries[:, first : first + 2 * HEAD],
            key_rows[:, first : first + 2 * HEAD],
            values[:, first : first + 2 * HEAD],
            log_totals[pair_index : pair_index + 2],
            grad_rows[:, first : first + 2 * HEAD],
        )
        query_parts.append(grad_query)
        key_parts.append(grad_key)
        value_parts.append(grad_value)
    return (
        jnp.concatenate(query_parts, axis=1),
        jnp.concatenate(key_parts, axis=1),
        jnp.concatenate(value_parts, axis=1),
    )


def swap_with(values, axis, size, bit):
    return lax.ppermute(values, axis, [(index, index ^ (1 << bit)) for index in range(size)])


def own_bit(axis, bit):
    return (lax.axis_index(axis) >> bit) & 1


def join_pair(values, axis, size, bit, place):
    other = swap_with(values, axis, size, bit)
    low = own_bit(axis, bit) == 0
    return jnp.stack([jnp.where(low, values, other), jnp.where(low, other, values)], axis=place)


def bit_orders(size):
    upper = list(range(1, size.bit_length() - 1))
    return (upper, upper[::-1])


def spread(part, axis, size, order):
    done = []
    for bit in order:
        part = join_pair(part, axis, size, bit, sum(1 for seen in done if seen > bit))
        done.append(bit)
    return part


def gather_rows(part, axis, size):
    rows, columns = part.shape
    half = columns // 2
    first, second = bit_orders(size)
    joined = jnp.concatenate(
        [spread(part[:, :half], axis, size, first), spread(part[:, half:], axis, size, second)],
        axis=-1,
    )
    joined = join_pair(joined, axis, size, 0, size.bit_length() - 2)
    return joined.reshape(size * rows, columns)


def halve(values, axis, size, bit, place):
    mine = own_bit(axis, bit)
    keep = lax.dynamic_index_in_dim(values, mine, place, keepdims=False)
    give = lax.dynamic_index_in_dim(values, 1 - mine, place, keepdims=False)
    other = swap_with(give, axis, size, bit)
    return keep.astype(jnp.float32) + other.astype(jnp.float32)


def scatter_part(values, axis, size, order):
    left = sorted(order, reverse=True)
    for bit in order:
        place = left.index(bit)
        values = halve(values, axis, size, bit, place).astype(jnp.bfloat16)
        left.remove(bit)
    return values


def reduce_grad(grad, fsdp, dp):
    rows, columns = (grad.shape[0] // fsdp, grad.shape[1])
    half = columns // 2
    count = fsdp.bit_length() - 1
    values = grad.astype(jnp.bfloat16).reshape((2,) * count + (rows, columns))
    values = halve(values, "fsdp", fsdp, 0, count - 1).astype(jnp.bfloat16)
    first, second = bit_orders(fsdp)
    left = scatter_part(values[..., :half], "fsdp", fsdp, first)
    right = scatter_part(values[..., half:], "fsdp", fsdp, second)
    low = own_bit("dp", 0) == 0
    keep = jnp.where(low, left, right)
    other = swap_with(jnp.where(low, right, left), "dp", dp, 0)
    total = keep.astype(jnp.float32) + other.astype(jnp.float32)
    upper = list(range(1, dp.bit_length() - 1))
    for bit in upper:
        pair = total.astype(jnp.bfloat16).reshape(2, total.shape[0] // 2, half)
        total = halve(pair, "dp", dp, bit, 0)
    total = lax.reduce_precision(total, 8, 7).astype(jnp.bfloat16)
    for bit in upper[::-1]:
        total = join_pair(total, "dp", dp, bit, 0).reshape(2 * total.shape[0], half)
    other = swap_with(total, "dp", dp, 0)
    return jnp.concatenate(
        [jnp.where(low, total, other), jnp.where(low, other, total)], axis=1
    ).astype(jnp.float32)


def gather_all(values, fsdp, dp):
    rounded = lax.reduce_precision(values, 8, 7).astype(jnp.bfloat16)
    over_dp = spread(rounded, "dp", dp, list(range(dp.bit_length() - 1)))
    both = spread(over_dp, "fsdp", fsdp, list(range(fsdp.bit_length() - 1))[::-1])
    return both.reshape((fsdp * dp,) + values.shape)


def own_block(values, axis, size):
    count = values.shape[0] // size
    return lax.dynamic_slice_in_dim(values, lax.axis_index(axis) * count, count, 0)


def lane_rows(vector):
    return jnp.pad(vector, (0, -vector.shape[0] % 128)).reshape(-1, 128)


def body(
    tokens,
    absorbed,
    noise_level,
    cotangent,
    level_table,
    absorb_vector,
    attn_gain,
    qkv_weight,
    out_weight,
    mlp_gain,
    up_weight,
    up_bias,
    down_weight,
    down_bias,
    mod_weight,
    mod_bias,
):
    fsdp = lax.axis_size("fsdp")
    dp = lax.axis_size("dp")
    small = (absorb_vector, attn_gain, mlp_gain, up_bias, down_bias, mod_bias)
    packed = jnp.concatenate([level_table] + [lane_rows(vector) for vector in small], axis=0)
    count = fsdp.bit_length() - 1
    packed = spread(packed, "fsdp", fsdp, list(range(count))[::-1])
    packed = packed.reshape((fsdp,) + packed.shape[count:])
    table_rows, temb = level_table.shape
    table_full = packed[:, :table_rows].reshape(fsdp * table_rows, temb)
    unpacked = []
    first = table_rows
    for vector in small:
        last = first + -(-vector.shape[0] // 128)
        rows = packed[:, first:last].reshape(fsdp, -1)[:, : vector.shape[0]]
        unpacked.append(rows.reshape(-1))
        first = last
    absorb_full, gain_attn, gain_mlp, up_bias_full, down_bias_full, mod_bias_full = unpacked
    mod_full = gather_rows(mod_weight, "fsdp", fsdp)
    qkv_full = gather_rows(qkv_weight, "fsdp", fsdp)
    out_full = gather_rows(out_weight, "fsdp", fsdp)
    up_full = gather_rows(up_weight, "fsdp", fsdp)
    down_full = gather_rows(down_weight, "fsdp", fsdp)
    seq_count = noise_level.shape[0]
    row_count, model_width = tokens.shape
    length = row_count // seq_count
    head_count = model_width // HEAD
    levels = table_full.shape[0]
    level_picks = (jnp.arange(levels)[None, :] == noise_level[:, None]).astype(jnp.bfloat16)
    embedded = product(level_picks, table_full)
    cond_low = jax.nn.silu(embedded).astype(jnp.bfloat16)
    modulation = product(cond_low, mod_full) + mod_bias_full.astype(jnp.float32)
    pieces = jnp.split(modulation, 6, axis=1)
    shift_one, scale_one, gate_one, shift_two, scale_two, gate_two = [
        piece[:, None, :] for piece in pieces
    ]
    absorbed_rows = (absorbed > 0).reshape(seq_count, length, 1)
    start_rows = jnp.where(
        absorbed_rows,
        absorb_full.astype(jnp.float32)[None, None, :],
        tokens.astype(jnp.float32).reshape(seq_count, length, model_width),
    )
    gain_one = gain_attn.astype(jnp.float32)
    unit_one, inverse_one = normalize(start_rows)
    hidden_one = (
        (unit_one * gain_one * (1.0 + scale_one) + shift_one)
        .astype(jnp.bfloat16)
        .reshape(row_count, model_width)
    )
    projected = product(hidden_one, qkv_full).reshape(seq_count, length, 3, head_count, HEAD)
    cosine, sine = rotary(length, HEAD)
    queries = (
        rotate(projected[:, :, 0], cosine, sine)
        .astype(jnp.bfloat16)
        .reshape(seq_count, length, model_width)
    )
    key_rows = (
        rotate(projected[:, :, 1], cosine, sine)
        .astype(jnp.bfloat16)
        .reshape(seq_count, length, model_width)
    )
    values = projected[:, :, 2].astype(jnp.bfloat16).reshape(seq_count, length, model_width)
    mixed_rows, log_totals = lax.map(sequence_forward, (queries, key_rows, values))
    mixed_flat = mixed_rows.reshape(row_count, model_width)
    attended = product(mixed_flat, out_full).reshape(seq_count, length, model_width)
    middle = start_rows + gate_one * attended
    gain_two = gain_mlp.astype(jnp.float32)
    unit_two, inverse_two = normalize(middle)
    hidden_two = (
        (unit_two * gain_two * (1.0 + scale_two) + shift_two)
        .astype(jnp.bfloat16)
        .reshape(row_count, model_width)
    )
    up_values = product(hidden_two, up_full) + up_bias_full.astype(jnp.float32)
    activated = jax.nn.gelu(up_values, approximate=True).astype(jnp.bfloat16)
    branch = (product(activated, down_full) + down_bias_full.astype(jnp.float32)).reshape(
        seq_count, length, model_width
    )
    block_out = (middle + gate_two * branch).reshape(row_count, model_width).astype(jnp.bfloat16)
    grad_out = cotangent.astype(jnp.float32).reshape(seq_count, length, model_width)
    d_gate_two = jnp.sum(grad_out * branch, axis=1)
    d_branch = (grad_out * gate_two).astype(jnp.bfloat16).reshape(row_count, model_width)
    g_down_bias = jnp.sum(d_branch.astype(jnp.float32), axis=0)
    g_down = reduce_grad(product_left(activated, d_branch), fsdp, dp)
    d_up = (product_right(d_branch, down_full) * gelu_slope(up_values)).astype(jnp.bfloat16)
    g_up_bias = jnp.sum(d_up.astype(jnp.float32), axis=0)
    g_up = reduce_grad(product_left(hidden_two, d_up), fsdp, dp)
    d_hid_two = product_right(d_up, up_full).reshape(seq_count, length, model_width)
    d_shift_two = jnp.sum(d_hid_two, axis=1)
    d_scale_two = jnp.sum(d_hid_two * unit_two * gain_two, axis=1)
    g_gain_two = jnp.sum(d_hid_two * unit_two * (1.0 + scale_two), axis=(0, 1))
    d_middle = grad_out + norm_back(d_hid_two * gain_two * (1.0 + scale_two), unit_two, inverse_two)
    d_gate_one = jnp.sum(d_middle * attended, axis=1)
    d_attended = (d_middle * gate_one).astype(jnp.bfloat16).reshape(row_count, model_width)
    g_out = reduce_grad(product_left(mixed_flat, d_attended), fsdp, dp)
    d_mixed = (
        product_right(d_attended, out_full)
        .astype(jnp.bfloat16)
        .reshape(seq_count, length, model_width)
    )
    d_queries, d_keys, d_values = lax.map(
        sequence_backward, (queries, key_rows, values, log_totals, d_mixed)
    )
    head_shape = (seq_count, length, head_count, HEAD)
    d_queries = rotate_back(d_queries.reshape(head_shape), cosine, sine)
    d_keys = rotate_back(d_keys.reshape(head_shape), cosine, sine)
    d_projected = jnp.stack([d_queries, d_keys, d_values.reshape(head_shape)], axis=2)
    d_projected = d_projected.reshape(row_count, 3 * model_width).astype(jnp.bfloat16)
    g_qkv = reduce_grad(product_left(hidden_one, d_projected), fsdp, dp)
    d_hid_one = product_right(d_projected, qkv_full).reshape(seq_count, length, model_width)
    d_shift_one = jnp.sum(d_hid_one, axis=1)
    d_scale_one = jnp.sum(d_hid_one * unit_one * gain_one, axis=1)
    g_gain_one = jnp.sum(d_hid_one * unit_one * (1.0 + scale_one), axis=(0, 1))
    d_start = d_middle + norm_back(d_hid_one * gain_one * (1.0 + scale_one), unit_one, inverse_one)
    tokens_grad = (
        jnp.where(absorbed_rows, 0.0, d_start).reshape(row_count, model_width).astype(jnp.bfloat16)
    )
    g_absorb = jnp.sum(jnp.where(absorbed_rows, d_start, 0.0), axis=(0, 1))
    width = model_width
    level_rows = jnp.broadcast_to(noise_level.astype(jnp.float32)[:, None], (seq_count, temb))
    early = jnp.concatenate(
        [d_gate_one, d_shift_two, d_scale_two, d_gate_two, embedded, level_rows], axis=1
    )
    early_sums = jnp.concatenate([g_gain_two, g_up_bias, g_down_bias])[None, :]
    late = jnp.concatenate([d_shift_one, d_scale_one], axis=1)
    late_sums = jnp.concatenate([g_gain_one, g_absorb])[None, :]
    early_all = gather_all(jnp.concatenate([early, jnp.broadcast_to(early_sums / seq_count, (seq_count, early_sums.shape[1]))], axis=1), fsdp, dp)
    late_all = gather_all(jnp.concatenate([late, jnp.broadcast_to(late_sums / seq_count, (seq_count, late_sums.shape[1]))], axis=1), fsdp, dp)
    early_all = early_all.reshape(-1, early_all.shape[-1])
    late_all = late_all.reshape(-1, late_all.shape[-1])
    d_mod = jnp.concatenate([late_all[:, : 2 * width], early_all[:, : 4 * width]], axis=1)
    embedded_all = early_all[:, 4 * width : 4 * width + temb].astype(jnp.float32)
    level_all = early_all[:, 4 * width + temb : 4 * width + temb + 1].astype(jnp.int32)
    early_totals = jnp.sum(early_all[:, 4 * width + 2 * temb :].astype(jnp.float32), axis=0)
    late_totals = jnp.sum(late_all[:, 2 * width :].astype(jnp.float32), axis=0)
    ff_width = up_bias_full.shape[0]
    g_gain_two = own_block(early_totals[:width], "fsdp", fsdp)
    g_up_bias = own_block(early_totals[width : width + ff_width], "fsdp", fsdp)
    g_down_bias = own_block(early_totals[width + ff_width :], "fsdp", fsdp)
    g_gain_one = own_block(late_totals[:width], "fsdp", fsdp)
    g_absorb = own_block(late_totals[width:], "fsdp", fsdp)
    cond_all = jax.nn.silu(embedded_all).astype(jnp.bfloat16)
    g_mod_bias = own_block(jnp.sum(d_mod.astype(jnp.float32), axis=0), "fsdp", fsdp)
    cond_own = lax.dynamic_slice_in_dim(
        cond_all, lax.axis_index("fsdp") * mod_weight.shape[0], mod_weight.shape[0], 1
    )
    g_mod = product_left(cond_own, d_mod)
    d_cond = product_right(d_mod, mod_full)
    sigmoid_of = jax.nn.sigmoid(embedded_all)
    d_embedded = d_cond * sigmoid_of * (1.0 + embedded_all * (1.0 - sigmoid_of))
    own_levels = lax.axis_index("fsdp") * table_rows + jnp.arange(table_rows)
    g_table = lax.dot_general(
        (level_all == own_levels[None, :]).astype(jnp.float32),
        d_embedded,
        (((0,), (0,)), ((), ())),
        precision=lax.Precision.HIGHEST,
    )
    owned_grads = (
        g_table,
        g_absorb,
        g_gain_one,
        g_qkv,
        g_out,
        g_gain_two,
        g_up,
        g_up_bias,
        g_down,
        g_down_bias,
        g_mod,
        g_mod_bias,
    )
    return (block_out, tokens_grad) + owned_grads


def solution(mesh):
    return jax.shard_map(
        body,
        mesh=mesh,
        in_specs=(
            P(("fsdp", "dp"), None),
            P(("fsdp", "dp")),
            P(("fsdp", "dp")),
            P(("fsdp", "dp"), None),
            P("fsdp", None),
            P("fsdp"),
            P("fsdp"),
            P("fsdp", None),
            P("fsdp", None),
            P("fsdp"),
            P("fsdp", None),
            P("fsdp"),
            P("fsdp", None),
            P("fsdp"),
            P("fsdp", None),
            P("fsdp"),
        ),
        out_specs=(
            P(("fsdp", "dp"), None),
            P(("fsdp", "dp"), None),
            P("fsdp", None),
            P("fsdp"),
            P("fsdp"),
            P("fsdp", None),
            P("fsdp", None),
            P("fsdp"),
            P("fsdp", None),
            P("fsdp"),
            P("fsdp", None),
            P("fsdp"),
            P("fsdp", None),
            P("fsdp"),
        ),
        check_vma=False,
    )
```

```python
import jax
import jax.numpy as jnp
from jax import lax
from jax.experimental import pallas as pl
from jax.experimental.pallas import tpu as pltpu
from jax.sharding import PartitionSpec as P

HEAD = 64
LANES = 2 * HEAD
CHUNK = 512
GROUPS = 3
VMEM_BYTES = 48 * 1024 * 1024


EPSILON = 1e-05
ROOT_TERM = 0.7978845608028654
CUBIC_TERM = 0.044715


def product(left, right):
    return jnp.dot(left, right, preferred_element_type=jnp.float32)


def product_left(left, right):
    return lax.dot_general(
        left, right, (((0,), (0,)), ((), ())), preferred_element_type=jnp.float32
    )


def product_right(left, right):
    return lax.dot_general(
        left, right, (((1,), (1,)), ((), ())), preferred_element_type=jnp.float32
    )


def normalize(values):
    centred = values - jnp.mean(values, axis=-1, keepdims=True)
    inverse = lax.rsqrt(jnp.mean(centred * centred, axis=-1, keepdims=True) + EPSILON)
    return (centred * inverse, inverse)


def norm_back(grads, unit_rows, inverse):
    return inverse * (
        grads
        - jnp.mean(grads, axis=-1, keepdims=True)
        - unit_rows * jnp.mean(grads * unit_rows, axis=-1, keepdims=True)
    )


def rotary(length):
    half_size = HEAD // 2
    inverse = 10000.0 ** (-2.0 * jnp.arange(half_size, dtype=jnp.float32) / HEAD)
    angles = jnp.arange(length, dtype=jnp.float32)[:, None] * inverse[None, :]
    angles = jnp.concatenate([angles] * (LANES // half_size), axis=1)
    return (jnp.cos(angles), jnp.sin(angles))


def gelu_slope(up_values):
    tanh_term = jnp.tanh(ROOT_TERM * (up_values + CUBIC_TERM * up_values * up_values * up_values))
    return 0.5 * (1.0 + tanh_term) + 0.5 * up_values * (1.0 - tanh_term * tanh_term) * ROOT_TERM * (
        1.0 + 3.0 * CUBIC_TERM * up_values * up_values
    )


def contract(left, right, left_dim, right_dim):
    return lax.dot_general(
        left,
        right,
        (((left_dim,), (right_dim,)), ((), ())),
        preferred_element_type=jnp.float32,
    )


def turn_lanes(values, sign):
    lane = lax.broadcasted_iota(jnp.int32, values.shape, 1)
    half_size = HEAD // 2
    ahead = pltpu.roll(values, LANES - half_size, 1)
    behind = pltpu.roll(values, half_size, 1)
    return jnp.where((lane & (HEAD - 1)) < half_size, -sign * ahead, sign * behind)


def head_lanes(values, head):
    lane = lax.broadcasted_iota(jnp.int32, values.shape, 1)
    wide = values.astype(jnp.float32)
    return jnp.where((lane >= HEAD) == (head == 1), wide, 0.0)


def attend_kernel(projected_ref, cosine_ref, sine_ref, turned_ref, mixed_ref, logs_ref):
    length = projected_ref.shape[0]
    cosine = cosine_ref[...]
    sine = sine_ref[...]
    for part in range(2):
        block = projected_ref[:, part * LANES : (part + 1) * LANES]
        turned = block * cosine + turn_lanes(block, 1.0) * sine
        turned_ref[:, part * LANES : (part + 1) * LANES] = turned.astype(jnp.bfloat16)
    turned_ref[:, 2 * LANES :] = projected_ref[:, 2 * LANES :].astype(jnp.bfloat16)
    key_rows = turned_ref[:, LANES : 2 * LANES]
    values = turned_ref[:, 2 * LANES :]
    for first in range(0, length, CHUNK):
        last = first + CHUNK
        outputs = []
        for head in range(2):
            queries = (head_lanes(turned_ref[first:last, :LANES], head) * HEAD ** (-0.5)).astype(
                jnp.bfloat16
            )
            scores = contract(key_rows, queries, 1, 1)
            highest = jnp.max(scores, axis=0, keepdims=True)
            exponent = jnp.exp(scores - highest)
            totals = jnp.sum(exponent, axis=0, keepdims=True)
            probs_low = (exponent * (1.0 / totals)).astype(jnp.bfloat16)
            outputs.append(contract(values, probs_low, 0, 0))
            logs_ref[0, head : head + 1, first:last] = highest + jnp.log(totals)
        row = lax.broadcasted_iota(jnp.int32, outputs[0].shape, 0)
        mixed = jnp.where(row < HEAD, outputs[0], outputs[1])
        mixed_ref[first:last, :] = mixed.T.astype(jnp.bfloat16)


def attend_back_kernel(turned_ref, mixed_grad_ref, logs_ref, cosine_ref, sine_ref, grad_ref):
    length = turned_ref.shape[0]
    key_rows = turned_ref[:, LANES : 2 * LANES]
    values = turned_ref[:, 2 * LANES :]
    head_keys = [head_lanes(key_rows, head).astype(jnp.bfloat16) for head in range(2)]
    key_grads = jnp.zeros((length, LANES), jnp.float32)
    value_grads = jnp.zeros((length, LANES), jnp.float32)
    for first in range(0, length, CHUNK):
        last = first + CHUNK
        query_grads = jnp.zeros((LANES, CHUNK), jnp.float32)
        for head in range(2):
            queries = (head_lanes(turned_ref[first:last, :LANES], head) * HEAD ** (-0.5)).astype(
                jnp.bfloat16
            )
            grad_heads = head_lanes(mixed_grad_ref[first:last, :], head).astype(jnp.bfloat16)
            scores = contract(key_rows, queries, 1, 1)
            probs = jnp.exp(scores - logs_ref[0, head : head + 1, first:last])
            grad_probs = contract(values, grad_heads, 1, 1)
            value_grads += contract(probs.astype(jnp.bfloat16), grad_heads, 1, 0)
            weighted = probs * grad_probs
            grad_scores = (
                weighted - probs * jnp.sum(weighted, axis=0, keepdims=True)
            ).astype(jnp.bfloat16)
            key_grads += contract(grad_scores, queries, 1, 0)
            query_grads += contract(head_keys[head], grad_scores, 0, 0)
        turned = query_grads.T * HEAD ** (-0.5)
        grad_ref[first:last, :LANES] = (
            turned * cosine_ref[first:last, :] - turn_lanes(turned * sine_ref[first:last, :], 1.0)
        ).astype(jnp.bfloat16)
    grad_ref[:, LANES : 2 * LANES] = (
        key_grads * cosine_ref[...] - turn_lanes(key_grads * sine_ref[...], 1.0)
    ).astype(jnp.bfloat16)
    grad_ref[:, 2 * LANES :] = value_grads.astype(jnp.bfloat16)


def attend(projected, cosine, sine, group, pairs, length):
    rows = projected.shape[0]
    seq_count = rows // length
    wide = 3 * LANES
    table = pl.BlockSpec((length, LANES), lambda seq, pair: (0, 0))
    return pl.pallas_call(
        attend_kernel,
        grid=(seq_count, pairs),
        in_specs=[
            pl.BlockSpec((length, wide), lambda seq, pair: (seq, group * pairs + pair)),
            table,
            table,
        ],
        out_specs=[
            pl.BlockSpec((length, wide), lambda seq, pair: (seq, pair)),
            pl.BlockSpec((length, LANES), lambda seq, pair: (seq, pair)),
            pl.BlockSpec((1, 8, length), lambda seq, pair: (seq * pairs + pair, 0, 0)),
        ],
        out_shape=[
            jax.ShapeDtypeStruct((rows, pairs * wide), jnp.bfloat16),
            jax.ShapeDtypeStruct((rows, pairs * LANES), jnp.bfloat16),
            jax.ShapeDtypeStruct((seq_count * pairs, 8, length), jnp.float32),
        ],
        compiler_params=pltpu.CompilerParams(vmem_limit_bytes=VMEM_BYTES),
        cost_estimate=pl.CostEstimate(
            flops=rows * length * pairs * LANES * 16,
            transcendentals=rows * length * pairs * 2,
            bytes_accessed=rows * pairs * wide * 8,
        ),
        name="attend",
    )(projected, cosine, sine)


def attend_back(turned, mixed_grad, logs, cosine, sine, group, pairs, length):
    rows = turned.shape[0]
    seq_count = rows // length
    wide = 3 * LANES
    table = pl.BlockSpec((length, LANES), lambda seq, pair: (0, 0))
    return pl.pallas_call(
        attend_back_kernel,
        grid=(seq_count, pairs),
        in_specs=[
            pl.BlockSpec((length, wide), lambda seq, pair: (seq, pair)),
            pl.BlockSpec((length, LANES), lambda seq, pair: (seq, group * pairs + pair)),
            pl.BlockSpec((1, 8, length), lambda seq, pair: (seq * pairs + pair, 0, 0)),
            table,
            table,
        ],
        out_specs=pl.BlockSpec((length, wide), lambda seq, pair: (seq, pair)),
        out_shape=jax.ShapeDtypeStruct((rows, pairs * wide), jnp.bfloat16),
        compiler_params=pltpu.CompilerParams(vmem_limit_bytes=VMEM_BYTES),
        cost_estimate=pl.CostEstimate(
            flops=rows * length * pairs * LANES * 40,
            transcendentals=rows * length * pairs * 2,
            bytes_accessed=rows * pairs * wide * 8,
        ),
        name="attend_back",
    )(turned, mixed_grad, logs, cosine, sine)


def swap_with(values, axis, size, bit):
    return lax.ppermute(values, axis, [(index, index ^ (1 << bit)) for index in range(size)])


def own_bit(axis, bit):
    return (lax.axis_index(axis) >> bit) & 1


def join_pair(values, axis, size, bit, place):
    other = swap_with(values, axis, size, bit)
    low = own_bit(axis, bit) == 0
    return jnp.stack([jnp.where(low, values, other), jnp.where(low, other, values)], axis=place)


def bit_orders(size):
    upper = list(range(1, size.bit_length() - 1))
    return (upper, upper[::-1])


def spread(part, axis, size, order):
    done = []
    for bit in order:
        part = join_pair(part, axis, size, bit, sum(1 for seen in done if seen > bit))
        done.append(bit)
    return part


class Chain:
    def __init__(self, steps):
        self.steps = steps
        self.result = None
        self.pending = next(steps)

    def step(self, arrived):
        try:
            self.pending = self.steps.send(arrived)
        except StopIteration as end:
            self.pending = None
            self.result = end.value

    def finish(self):
        while self.pending is not None:
            self.step(self.pending)
        return self.result


def advance(held, *chains):
    chains = [chain for chain in chains if chain.pending is not None]
    flat, shape = jax.tree.flatten((held, [chain.pending for chain in chains]))
    held, arrived = jax.tree.unflatten(shape, lax.optimization_barrier(flat))
    for chain, results in zip(chains, arrived):
        chain.step(results)
    return held


def merge(values, other, axis, bit, place):
    low = own_bit(axis, bit) == 0
    return jnp.stack([jnp.where(low, values, other), jnp.where(low, other, values)], axis=place)


def gather_steps(part, size):
    rows, columns = part.shape
    half = columns // 2
    left, right = (part[:, :half], part[:, half:])
    first, second = bit_orders(size)
    done = ([], [])
    for bits in zip(first, second):
        others = yield [
            swap_with(left, "fsdp", size, bits[0]),
            swap_with(right, "fsdp", size, bits[1]),
        ]
        places = [sum(1 for seen in old if seen > bit) for old, bit in zip(done, bits)]
        left = merge(left, others[0], "fsdp", bits[0], places[0])
        right = merge(right, others[1], "fsdp", bits[1], places[1])
        done[0].append(bits[0])
        done[1].append(bits[1])
    joined = jnp.concatenate([left, right], axis=-1)
    others = yield [swap_with(joined, "fsdp", size, 0)]
    joined = merge(joined, others[0], "fsdp", 0, size.bit_length() - 2)
    return joined.reshape(size * rows, columns)


def two_parts(values, axis, bit, place):
    mine = own_bit(axis, bit)
    keep = lax.dynamic_index_in_dim(values, mine, place, keepdims=False)
    give = lax.dynamic_index_in_dim(values, 1 - mine, place, keepdims=False)
    return (keep, give)


def add_low(keep, other):
    return (keep.astype(jnp.float32) + other.astype(jnp.float32)).astype(jnp.bfloat16)


def reduce_steps(grad, fsdp, dp):
    rows, columns = (grad.shape[0] // fsdp, grad.shape[1])
    half = columns // 2
    count = fsdp.bit_length() - 1
    values = grad.astype(jnp.bfloat16).reshape((2,) * count + (rows, columns))
    keep, give = two_parts(values, "fsdp", 0, count - 1)
    others = yield [swap_with(give, "fsdp", fsdp, 0)]
    values = add_low(keep, others[0])
    halves = [values[..., :half], values[..., half:]]
    left = [list(range(count - 1, 0, -1)) for _ in halves]
    for bits in zip(*bit_orders(fsdp)):
        pairs = [
            two_parts(values, "fsdp", bit, rest.index(bit))
            for values, bit, rest in zip(halves, bits, left)
        ]
        others = yield [
            swap_with(give, "fsdp", fsdp, bit) for (_, give), bit in zip(pairs, bits)
        ]
        halves = [add_low(keep, other) for (keep, _), other in zip(pairs, others)]
        for rest, bit in zip(left, bits):
            rest.remove(bit)
    low = own_bit("dp", 0) == 0
    keep = jnp.where(low, halves[0], halves[1])
    give = jnp.where(low, halves[1], halves[0])
    upper = list(range(1, dp.bit_length() - 1))
    for bit in [0] + upper:
        if bit > 0:
            pair = total.astype(jnp.bfloat16).reshape(2, total.shape[0] // 2, half)
            keep, give = two_parts(pair, "dp", bit, 0)
        others = yield [swap_with(give, "dp", dp, bit)]
        total = keep.astype(jnp.float32) + others[0].astype(jnp.float32)
    total = lax.reduce_precision(total, 8, 7).astype(jnp.bfloat16)
    for bit in upper[::-1]:
        others = yield [swap_with(total, "dp", dp, bit)]
        total = merge(total, others[0], "dp", bit, 0).reshape(2 * total.shape[0], half)
    others = yield [swap_with(total, "dp", dp, 0)]
    return jnp.concatenate(
        [jnp.where(low, total, others[0]), jnp.where(low, others[0], total)], axis=1
    ).astype(jnp.float32)


def share_steps(values, fsdp, dp):
    shape = values.shape
    values = lax.reduce_precision(values, 8, 7).astype(jnp.bfloat16)
    for axis, size in (("dp", dp), ("fsdp", fsdp)):
        for bit in range(size.bit_length() - 1):
            others = yield [swap_with(values, axis, size, bit)]
            values = merge(values, others[0], axis, bit, 0).reshape((-1,) + shape[1:])
    return values


def own_block(values, axis, size):
    count = values.shape[0] // size
    return lax.dynamic_slice_in_dim(values, lax.axis_index(axis) * count, count, 0)


def lane_rows(vector):
    return jnp.pad(vector, (0, -vector.shape[0] % 128)).reshape(-1, 128)


def body(
    tokens,
    absorbed,
    noise_level,
    cotangent,
    level_table,
    absorb_vector,
    attn_gain,
    qkv_weight,
    out_weight,
    mlp_gain,
    up_weight,
    up_bias,
    down_weight,
    down_bias,
    mod_weight,
    mod_bias,
):
    fsdp = lax.axis_size("fsdp")
    dp = lax.axis_size("dp")
    small = (absorb_vector, attn_gain, mlp_gain, up_bias, down_bias, mod_bias)
    packed = jnp.concatenate([level_table] + [lane_rows(vector) for vector in small], axis=0)
    count = fsdp.bit_length() - 1
    packed = spread(packed, "fsdp", fsdp, list(range(count))[::-1])
    packed = packed.reshape((fsdp,) + packed.shape[count:])
    table_rows, temb = level_table.shape
    table_full = packed[:, :table_rows].reshape(fsdp * table_rows, temb)
    unpacked = []
    first = table_rows
    for vector in small:
        last = first + -(-vector.shape[0] // 128)
        rows = packed[:, first:last].reshape(fsdp, -1)[:, : vector.shape[0]]
        unpacked.append(rows.reshape(-1))
        first = last
    absorb_full, gain_attn, gain_mlp, up_bias_full, down_bias_full, mod_bias_full = unpacked
    model_width = tokens.shape[1]
    pair_count = model_width // LANES
    paired = qkv_weight.reshape(-1, 3, pair_count, LANES).swapaxes(1, 2)
    qkv_chain = Chain(gather_steps(paired.reshape(qkv_weight.shape), fsdp))
    mod_full = Chain(gather_steps(mod_weight, fsdp)).finish()
    for _ in range(count - 1):
        out_weight, up_weight, down_weight = advance(
            (out_weight, up_weight, down_weight), qkv_chain
        )
    out_chain = Chain(gather_steps(out_weight, fsdp))
    up_chain = Chain(gather_steps(up_weight, fsdp))
    down_chain = Chain(gather_steps(down_weight, fsdp))
    qkv_full = qkv_chain.finish()
    seq_count = noise_level.shape[0]
    row_count = tokens.shape[0]
    length = row_count // seq_count
    levels = table_full.shape[0]
    level_picks = (jnp.arange(levels)[None, :] == noise_level[:, None]).astype(jnp.bfloat16)
    embedded = product(level_picks, table_full)
    cond_low = jax.nn.silu(embedded).astype(jnp.bfloat16)
    modulation = product(cond_low, mod_full) + mod_bias_full.astype(jnp.float32)
    pieces = jnp.split(modulation, 6, axis=1)
    shift_one, scale_one, gate_one, shift_two, scale_two, gate_two = [
        piece[:, None, :] for piece in pieces
    ]
    absorbed_rows = (absorbed > 0).reshape(seq_count, length, 1)
    start_rows = jnp.where(
        absorbed_rows,
        absorb_full.astype(jnp.float32)[None, None, :],
        tokens.astype(jnp.float32).reshape(seq_count, length, model_width),
    )
    gain_one = gain_attn.astype(jnp.float32)
    unit_one, inverse_one = normalize(start_rows)
    hidden_one = (
        (unit_one * gain_one * (1.0 + scale_one) + shift_one)
        .astype(jnp.bfloat16)
        .reshape(row_count, model_width)
    )
    projected = product(hidden_one, qkv_full)
    cosine, sine = rotary(length)
    groups = GROUPS if pair_count % GROUPS == 0 else 1
    group_pairs = pair_count // groups
    turned, mixed_parts, logs = ([], [], [])
    for group in range(groups):
        projected = advance(projected, out_chain, up_chain, *([down_chain] if group != 1 else []))
        parts = attend(projected, cosine, sine, group, group_pairs, length)
        turned.append(parts[0])
        mixed_parts.append(parts[1])
        logs.append(parts[2])
    mixed_flat = jnp.concatenate(mixed_parts, axis=1)
    out_full = out_chain.finish()
    up_full = up_chain.finish()
    mixed_flat = advance(mixed_flat, down_chain)
    attended = product(mixed_flat, out_full).reshape(seq_count, length, model_width)
    middle = start_rows + gate_one * attended
    gain_two = gain_mlp.astype(jnp.float32)
    unit_two, inverse_two = normalize(middle)
    hidden_two = (
        (unit_two * gain_two * (1.0 + scale_two) + shift_two)
        .astype(jnp.bfloat16)
        .reshape(row_count, model_width)
    )
    down_full = down_chain.finish()
    up_values = product(hidden_two, up_full) + up_bias_full.astype(jnp.float32)
    activated = jax.nn.gelu(up_values, approximate=True).astype(jnp.bfloat16)
    branch = (product(activated, down_full) + down_bias_full.astype(jnp.float32)).reshape(
        seq_count, length, model_width
    )
    block_out = (middle + gate_two * branch).reshape(row_count, model_width).astype(jnp.bfloat16)
    grad_out = cotangent.astype(jnp.float32).reshape(seq_count, length, model_width)
    d_gate_two = jnp.sum(grad_out * branch, axis=1)
    d_branch = (grad_out * gate_two).astype(jnp.bfloat16).reshape(row_count, model_width)
    g_down_bias = jnp.sum(d_branch.astype(jnp.float32), axis=0)
    down_sum = Chain(reduce_steps(product_left(activated, d_branch), fsdp, dp))
    d_up = (product_right(d_branch, down_full) * gelu_slope(up_values)).astype(jnp.bfloat16)
    d_up = advance(d_up, down_sum)
    g_up_bias = jnp.sum(d_up.astype(jnp.float32), axis=0)
    up_sum = Chain(reduce_steps(product_left(hidden_two, d_up), fsdp, dp))
    d_up = advance(d_up, down_sum)
    d_hid_two = product_right(d_up, up_full).reshape(seq_count, length, model_width)
    d_shift_two = jnp.sum(d_hid_two, axis=1)
    d_scale_two = jnp.sum(d_hid_two * unit_two * gain_two, axis=1)
    g_gain_two = jnp.sum(d_hid_two * unit_two * (1.0 + scale_two), axis=(0, 1))
    d_middle = grad_out + norm_back(d_hid_two * gain_two * (1.0 + scale_two), unit_two, inverse_two)
    d_gate_one = jnp.sum(d_middle * attended, axis=1)
    d_attended = (d_middle * gate_one).astype(jnp.bfloat16).reshape(row_count, model_width)
    d_attended = advance(d_attended, down_sum, up_sum)
    out_sum = Chain(reduce_steps(product_left(mixed_flat, d_attended), fsdp, dp))
    d_mixed = product_right(d_attended, out_full).astype(jnp.bfloat16)
    level_rows = jnp.broadcast_to(noise_level.astype(jnp.float32)[:, None], (seq_count, temb))
    early_sums = jnp.concatenate([g_gain_two, g_up_bias, g_down_bias])[None, :] / seq_count
    early = jnp.concatenate(
        [d_gate_one, d_shift_two, d_scale_two, d_gate_two, embedded, level_rows]
        + [jnp.broadcast_to(early_sums, (seq_count, early_sums.shape[1]))],
        axis=1,
    )
    early_chain = Chain(share_steps(early, fsdp, dp))
    open_sums = [down_sum, up_sum, out_sum, early_chain]
    qkv_sums = []
    d_hid_one = 0.0
    for group in range(groups):
        d_mixed = advance(d_mixed, *open_sums)
        d_group = attend_back(
            turned[group], d_mixed, logs[group], cosine, sine, group, group_pairs, length
        )
        qkv_sums.append(Chain(reduce_steps(product_left(hidden_one, d_group), fsdp, dp)))
        open_sums.append(qkv_sums[-1])
        columns = group_pairs * 3 * LANES
        part = qkv_full[:, group * columns : (group + 1) * columns]
        d_hid_one = d_hid_one + product_right(d_group, part)
    d_hid_one = advance(d_hid_one, *open_sums)
    d_hid_one = d_hid_one.reshape(seq_count, length, model_width)
    d_shift_one = jnp.sum(d_hid_one, axis=1)
    d_scale_one = jnp.sum(d_hid_one * unit_one * gain_one, axis=1)
    g_gain_one = jnp.sum(d_hid_one * unit_one * (1.0 + scale_one), axis=(0, 1))
    d_start = d_middle + norm_back(d_hid_one * gain_one * (1.0 + scale_one), unit_one, inverse_one)
    tokens_grad = (
        jnp.where(absorbed_rows, 0.0, d_start).reshape(row_count, model_width).astype(jnp.bfloat16)
    )
    g_absorb = jnp.sum(jnp.where(absorbed_rows, d_start, 0.0), axis=(0, 1))
    width = model_width
    late_sums = jnp.concatenate([g_gain_one, g_absorb])[None, :] / seq_count
    late = jnp.concatenate(
        [d_shift_one, d_scale_one, jnp.broadcast_to(late_sums, (seq_count, late_sums.shape[1]))],
        axis=1,
    )
    late_all = Chain(share_steps(late, fsdp, dp)).finish()
    early_all = early_chain.finish()
    g_down = down_sum.finish()
    g_up = up_sum.finish()
    g_out = out_sum.finish()
    g_qkv = jnp.concatenate([chain.finish() for chain in qkv_sums], axis=1)
    g_qkv = g_qkv.reshape(-1, pair_count, 3, LANES).swapaxes(1, 2).reshape(qkv_weight.shape)
    d_mod = jnp.concatenate([late_all[:, : 2 * width], early_all[:, : 4 * width]], axis=1)
    embedded_all = early_all[:, 4 * width : 4 * width + temb].astype(jnp.float32)
    level_all = early_all[:, 4 * width + temb : 4 * width + temb + 1].astype(jnp.int32)
    early_totals = jnp.sum(early_all[:, 4 * width + 2 * temb :].astype(jnp.float32), axis=0)
    late_totals = jnp.sum(late_all[:, 2 * width :].astype(jnp.float32), axis=0)
    ff_width = up_bias_full.shape[0]
    g_gain_two = own_block(early_totals[:width], "fsdp", fsdp)
    g_up_bias = own_block(early_totals[width : width + ff_width], "fsdp", fsdp)
    g_down_bias = own_block(early_totals[width + ff_width :], "fsdp", fsdp)
    g_gain_one = own_block(late_totals[:width], "fsdp", fsdp)
    g_absorb = own_block(late_totals[width:], "fsdp", fsdp)
    cond_all = jax.nn.silu(embedded_all).astype(jnp.bfloat16)
    g_mod_bias = own_block(jnp.sum(d_mod.astype(jnp.float32), axis=0), "fsdp", fsdp)
    cond_own = lax.dynamic_slice_in_dim(
        cond_all, lax.axis_index("fsdp") * mod_weight.shape[0], mod_weight.shape[0], 1
    )
    g_mod = product_left(cond_own, d_mod)
    d_cond = product_right(d_mod, mod_full)
    sigmoid_of = jax.nn.sigmoid(embedded_all)
    d_embedded = d_cond * sigmoid_of * (1.0 + embedded_all * (1.0 - sigmoid_of))
    own_levels = lax.axis_index("fsdp") * table_rows + jnp.arange(table_rows)
    g_table = lax.dot_general(
        (level_all == own_levels[None, :]).astype(jnp.float32),
        d_embedded,
        (((0,), (0,)), ((), ())),
        precision=lax.Precision.HIGHEST,
    )
    owned_grads = (
        g_table,
        g_absorb,
        g_gain_one,
        g_qkv,
        g_out,
        g_gain_two,
        g_up,
        g_up_bias,
        g_down,
        g_down_bias,
        g_mod,
        g_mod_bias,
    )
    return (block_out, tokens_grad) + owned_grads


def solution(mesh):
    return jax.shard_map(
        body,
        mesh=mesh,
        in_specs=(
            P(("fsdp", "dp"), None),
            P(("fsdp", "dp")),
            P(("fsdp", "dp")),
            P(("fsdp", "dp"), None),
            P("fsdp", None),
            P("fsdp"),
            P("fsdp"),
            P("fsdp", None),
            P("fsdp", None),
            P("fsdp"),
            P("fsdp", None),
            P("fsdp"),
            P("fsdp", None),
            P("fsdp"),
            P("fsdp", None),
            P("fsdp"),
        ),
        out_specs=(
            P(("fsdp", "dp"), None),
            P(("fsdp", "dp"), None),
            P("fsdp", None),
            P("fsdp"),
            P("fsdp"),
            P("fsdp", None),
            P("fsdp", None),
            P("fsdp"),
            P("fsdp", None),
            P("fsdp"),
            P("fsdp", None),
            P("fsdp"),
            P("fsdp", None),
            P("fsdp"),
        ),
        check_vma=False,
    )
```

```python
import jax
import jax.numpy as jnp
from jax import lax
from jax.experimental import pallas as pl
from jax.experimental.pallas import tpu as pltpu
from jax.sharding import PartitionSpec as P

HEAD = 64
LANES = 2 * HEAD
CHUNK = 512
VMEM_BYTES = 48 * 1024 * 1024


EPSILON = 1e-05
ROOT_TERM = 0.7978845608028654
CUBIC_TERM = 0.044715


def product(left, right):
    return jnp.dot(left, right, preferred_element_type=jnp.float32)


def product_left(left, right):
    return lax.dot_general(
        left, right, (((0,), (0,)), ((), ())), preferred_element_type=jnp.float32
    )


def product_right(left, right):
    return lax.dot_general(
        left, right, (((1,), (1,)), ((), ())), preferred_element_type=jnp.float32
    )


def normalize(values):
    centred = values - jnp.mean(values, axis=-1, keepdims=True)
    inverse = lax.rsqrt(jnp.mean(centred * centred, axis=-1, keepdims=True) + EPSILON)
    return (centred * inverse, inverse)


def norm_back(grads, unit_rows, inverse):
    return inverse * (
        grads
        - jnp.mean(grads, axis=-1, keepdims=True)
        - unit_rows * jnp.mean(grads * unit_rows, axis=-1, keepdims=True)
    )


def rotary(length):
    half_size = HEAD // 2
    inverse = 10000.0 ** (-2.0 * jnp.arange(half_size, dtype=jnp.float32) / HEAD)
    angles = jnp.arange(length, dtype=jnp.float32)[:, None] * inverse[None, :]
    angles = jnp.concatenate([angles] * (LANES // half_size), axis=1)
    return (jnp.cos(angles), jnp.sin(angles))


def gelu_slope(up_values):
    tanh_term = jnp.tanh(ROOT_TERM * (up_values + CUBIC_TERM * up_values * up_values * up_values))
    return 0.5 * (1.0 + tanh_term) + 0.5 * up_values * (1.0 - tanh_term * tanh_term) * ROOT_TERM * (
        1.0 + 3.0 * CUBIC_TERM * up_values * up_values
    )


def contract(left, right, left_dim, right_dim):
    return lax.dot_general(
        left,
        right,
        (((left_dim,), (right_dim,)), ((), ())),
        preferred_element_type=jnp.float32,
    )


def turn_lanes(values, sign):
    lane = lax.broadcasted_iota(jnp.int32, values.shape, 1)
    half_size = HEAD // 2
    ahead = pltpu.roll(values, LANES - half_size, 1)
    behind = pltpu.roll(values, half_size, 1)
    return jnp.where((lane & (HEAD - 1)) < half_size, -sign * ahead, sign * behind)


def head_lanes(values, head):
    lane = lax.broadcasted_iota(jnp.int32, values.shape, 1)
    wide = values.astype(jnp.float32)
    return jnp.where((lane >= HEAD) == (head == 1), wide, 0.0)


def attend_kernel(projected_ref, cosine_ref, sine_ref, turned_ref, mixed_ref, logs_ref):
    length = projected_ref.shape[0]
    cosine = cosine_ref[...]
    sine = sine_ref[...]
    for part in range(2):
        block = projected_ref[:, part * LANES : (part + 1) * LANES]
        turned = block * cosine + turn_lanes(block, 1.0) * sine
        turned_ref[:, part * LANES : (part + 1) * LANES] = turned.astype(jnp.bfloat16)
    turned_ref[:, 2 * LANES :] = projected_ref[:, 2 * LANES :].astype(jnp.bfloat16)
    key_rows = turned_ref[:, LANES : 2 * LANES]
    values = turned_ref[:, 2 * LANES :]
    for first in range(0, length, CHUNK):
        last = first + CHUNK
        outputs = []
        for head in range(2):
            queries = (head_lanes(turned_ref[first:last, :LANES], head) * HEAD ** (-0.5)).astype(
                jnp.bfloat16
            )
            scores = contract(key_rows, queries, 1, 1)
            highest = jnp.max(scores, axis=0, keepdims=True)
            exponent = jnp.exp(scores - highest)
            totals = jnp.sum(exponent, axis=0, keepdims=True)
            probs_low = (exponent * (1.0 / totals)).astype(jnp.bfloat16)
            outputs.append(contract(values, probs_low, 0, 0))
            logs_ref[0, head : head + 1, first:last] = highest + jnp.log(totals)
        row = lax.broadcasted_iota(jnp.int32, outputs[0].shape, 0)
        mixed = jnp.where(row < HEAD, outputs[0], outputs[1])
        mixed_ref[first:last, :] = mixed.T.astype(jnp.bfloat16)


def attend_back_kernel(turned_ref, mixed_grad_ref, logs_ref, cosine_ref, sine_ref, grad_ref):
    length = turned_ref.shape[0]
    key_rows = turned_ref[:, LANES : 2 * LANES]
    values = turned_ref[:, 2 * LANES :]
    head_keys = [head_lanes(key_rows, head).astype(jnp.bfloat16) for head in range(2)]
    key_grads = jnp.zeros((length, LANES), jnp.float32)
    value_grads = jnp.zeros((length, LANES), jnp.float32)
    for first in range(0, length, CHUNK):
        last = first + CHUNK
        query_grads = jnp.zeros((LANES, CHUNK), jnp.float32)
        for head in range(2):
            queries = (head_lanes(turned_ref[first:last, :LANES], head) * HEAD ** (-0.5)).astype(
                jnp.bfloat16
            )
            grad_heads = head_lanes(mixed_grad_ref[first:last, :], head).astype(jnp.bfloat16)
            scores = contract(key_rows, queries, 1, 1)
            probs = jnp.exp(scores - logs_ref[0, head : head + 1, first:last])
            grad_probs = contract(values, grad_heads, 1, 1)
            value_grads += contract(probs.astype(jnp.bfloat16), grad_heads, 1, 0)
            weighted = probs * grad_probs
            grad_scores = (
                weighted - probs * jnp.sum(weighted, axis=0, keepdims=True)
            ).astype(jnp.bfloat16)
            key_grads += contract(grad_scores, queries, 1, 0)
            query_grads += contract(head_keys[head], grad_scores, 0, 0)
        turned = query_grads.T * HEAD ** (-0.5)
        grad_ref[first:last, :LANES] = (
            turned * cosine_ref[first:last, :] - turn_lanes(turned * sine_ref[first:last, :], 1.0)
        ).astype(jnp.bfloat16)
    grad_ref[:, LANES : 2 * LANES] = (
        key_grads * cosine_ref[...] - turn_lanes(key_grads * sine_ref[...], 1.0)
    ).astype(jnp.bfloat16)
    grad_ref[:, 2 * LANES :] = value_grads.astype(jnp.bfloat16)


def attend(projected, cosine, sine, start, pairs, length):
    rows = projected.shape[0]
    seq_count = rows // length
    wide = 3 * LANES
    table = pl.BlockSpec((length, LANES), lambda seq, pair: (0, 0))
    return pl.pallas_call(
        attend_kernel,
        grid=(seq_count, pairs),
        in_specs=[
            pl.BlockSpec((length, wide), lambda seq, pair: (seq, start + pair)),
            table,
            table,
        ],
        out_specs=[
            pl.BlockSpec((length, wide), lambda seq, pair: (seq, pair)),
            pl.BlockSpec((length, LANES), lambda seq, pair: (seq, pair)),
            pl.BlockSpec((1, 8, length), lambda seq, pair: (seq * pairs + pair, 0, 0)),
        ],
        out_shape=[
            jax.ShapeDtypeStruct((rows, pairs * wide), jnp.bfloat16),
            jax.ShapeDtypeStruct((rows, pairs * LANES), jnp.bfloat16),
            jax.ShapeDtypeStruct((seq_count * pairs, 8, length), jnp.float32),
        ],
        compiler_params=pltpu.CompilerParams(vmem_limit_bytes=VMEM_BYTES),
        cost_estimate=pl.CostEstimate(
            flops=rows * length * pairs * LANES * 16,
            transcendentals=rows * length * pairs * 2,
            bytes_accessed=rows * pairs * wide * 8,
        ),
        name="attend",
    )(projected, cosine, sine)


def attend_back(turned, mixed_grad, logs, cosine, sine, start, pairs, length):
    rows = turned.shape[0]
    seq_count = rows // length
    wide = 3 * LANES
    table = pl.BlockSpec((length, LANES), lambda seq, pair: (0, 0))
    return pl.pallas_call(
        attend_back_kernel,
        grid=(seq_count, pairs),
        in_specs=[
            pl.BlockSpec((length, wide), lambda seq, pair: (seq, pair)),
            pl.BlockSpec((length, LANES), lambda seq, pair: (seq, start + pair)),
            pl.BlockSpec((1, 8, length), lambda seq, pair: (seq * pairs + pair, 0, 0)),
            table,
            table,
        ],
        out_specs=pl.BlockSpec((length, wide), lambda seq, pair: (seq, pair)),
        out_shape=jax.ShapeDtypeStruct((rows, pairs * wide), jnp.bfloat16),
        compiler_params=pltpu.CompilerParams(vmem_limit_bytes=VMEM_BYTES),
        cost_estimate=pl.CostEstimate(
            flops=rows * length * pairs * LANES * 40,
            transcendentals=rows * length * pairs * 2,
            bytes_accessed=rows * pairs * wide * 8,
        ),
        name="attend_back",
    )(turned, mixed_grad, logs, cosine, sine)


def swap_with(values, axis, size, bit):
    return lax.ppermute(values, axis, [(index, index ^ (1 << bit)) for index in range(size)])


def own_bit(axis, bit):
    return (lax.axis_index(axis) >> bit) & 1


def bit_orders(size):
    upper = list(range(1, size.bit_length() - 1))
    return (upper, upper[::-1])


class Chain:
    def __init__(self, steps):
        self.steps = steps
        self.result = None
        self.pending = next(steps)

    def step(self, arrived):
        try:
            self.pending = self.steps.send(arrived)
        except StopIteration as end:
            self.pending = None
            self.result = end.value

    def finish(self):
        while self.pending is not None:
            self.step(self.pending)
        return self.result


def advance(held, *chains):
    chains = [chain for chain in chains if chain.pending is not None]
    flat, shape = jax.tree.flatten((held, [chain.pending for chain in chains]))
    held, arrived = jax.tree.unflatten(shape, lax.optimization_barrier(flat))
    for chain, results in zip(chains, arrived):
        chain.step(results)
    return held


def merge(values, other, axis, bit, place):
    low = own_bit(axis, bit) == 0
    return jnp.stack([jnp.where(low, values, other), jnp.where(low, other, values)], axis=place)


def gather_steps(part, size, orders):
    rows, columns = part.shape
    shares = jnp.split(part, len(orders), axis=1)
    done = [[] for _ in orders]
    for bits in zip(*orders):
        others = yield [swap_with(share, "fsdp", size, bit) for share, bit in zip(shares, bits)]
        places = [sum(1 for seen in old if seen > bit) for old, bit in zip(done, bits)]
        shares = [
            merge(share, other, "fsdp", bit, place)
            for share, other, bit, place in zip(shares, others, bits, places)
        ]
        for old, bit in zip(done, bits):
            old.append(bit)
    joined = jnp.concatenate(shares, axis=-1)
    others = yield [swap_with(joined, "fsdp", size, 0)]
    joined = merge(joined, others[0], "fsdp", 0, size.bit_length() - 2)
    return joined.reshape(size * rows, columns)


def two_parts(values, axis, bit, place):
    mine = own_bit(axis, bit)
    keep = lax.dynamic_index_in_dim(values, mine, place, keepdims=False)
    give = lax.dynamic_index_in_dim(values, 1 - mine, place, keepdims=False)
    return (keep, give)


def add_low(keep, other):
    return (keep.astype(jnp.float32) + other.astype(jnp.float32)).astype(jnp.bfloat16)


def reduce_steps(grad, fsdp, dp, order, split):
    rows, columns = (grad.shape[0] // fsdp, grad.shape[1])
    count = fsdp.bit_length() - 1
    values = grad.astype(jnp.bfloat16).reshape((2,) * count + (rows, columns))
    left = list(range(count - 1, -1, -1))
    for bit in [0] + order:
        keep, give = two_parts(values, "fsdp", bit, left.index(bit))
        others = yield [swap_with(give, "fsdp", fsdp, bit)]
        values = add_low(keep, others[0])
        left.remove(bit)
    bits = list(range(dp.bit_length() - 1))
    if not split:
        for bit in bits:
            values = lax.reduce_precision(values.astype(jnp.float32), 8, 7).astype(jnp.bfloat16)
            others = yield [swap_with(values, "dp", dp, bit)]
            values = values.astype(jnp.float32) + others[0].astype(jnp.float32)
        return values
    half = columns // 2
    low = own_bit("dp", 0) == 0
    for bit in bits:
        if bit == 0:
            keep = jnp.where(low, values[:, :half], values[:, half:])
            give = jnp.where(low, values[:, half:], values[:, :half])
        else:
            pair = total.astype(jnp.bfloat16).reshape(2, total.shape[0] // 2, half)
            keep, give = two_parts(pair, "dp", bit, 0)
        others = yield [swap_with(give, "dp", dp, bit)]
        total = keep.astype(jnp.float32) + others[0].astype(jnp.float32)
    total = lax.reduce_precision(total, 8, 7).astype(jnp.bfloat16)
    for bit in bits[:0:-1]:
        others = yield [swap_with(total, "dp", dp, bit)]
        total = merge(total, others[0], "dp", bit, 0).reshape(2 * total.shape[0], half)
    others = yield [swap_with(total, "dp", dp, 0)]
    return jnp.concatenate(
        [jnp.where(low, total, others[0]), jnp.where(low, others[0], total)], axis=1
    ).astype(jnp.float32)


def share_steps(values, fsdp, dp):
    shape = values.shape
    values = lax.reduce_precision(values, 8, 7).astype(jnp.bfloat16)
    for bit in range(dp.bit_length() - 1):
        others = yield [swap_with(values, "dp", dp, bit)]
        values = merge(values, others[0], "dp", bit, 0)
    for place, bit in enumerate(range(fsdp.bit_length() - 2, -1, -1)):
        others = yield [swap_with(values, "fsdp", fsdp, bit)]
        values = merge(values, others[0], "fsdp", bit, place)
    return values.reshape((-1,) + shape[1:])


def own_block(values, axis, size):
    count = values.shape[0] // size
    return lax.dynamic_slice_in_dim(values, lax.axis_index(axis) * count, count, 0)


def lane_rows(vector):
    return jnp.pad(vector, (0, -vector.shape[0] % 128)).reshape(-1, 128)


def body(
    tokens,
    absorbed,
    noise_level,
    cotangent,
    level_table,
    absorb_vector,
    attn_gain,
    qkv_weight,
    out_weight,
    mlp_gain,
    up_weight,
    up_bias,
    down_weight,
    down_bias,
    mod_weight,
    mod_bias,
):
    fsdp = lax.axis_size("fsdp")
    dp = lax.axis_size("dp")
    small = (absorb_vector, attn_gain, mlp_gain, up_bias, down_bias, mod_bias)
    packed = jnp.concatenate([level_table] + [lane_rows(vector) for vector in small], axis=0)
    mod_rows, mod_columns = mod_weight.shape
    packed_rows = packed.shape[0]
    packed = jnp.pad(packed, ((0, -packed_rows % mod_rows), (0, 0))).reshape(mod_rows, -1)
    first_order, second_order = bit_orders(fsdp)
    pair_count = tokens.shape[1] // LANES
    paired = qkv_weight.reshape(-1, 3, pair_count, LANES).swapaxes(1, 2)
    qkv_chain = Chain(
        gather_steps(paired.reshape(qkv_weight.shape), fsdp, (first_order, second_order))
    )
    mod_packed = jnp.concatenate([mod_weight, packed], axis=1)
    mod_packed = Chain(gather_steps(mod_packed, fsdp, (first_order,))).finish()
    mod_full = mod_packed[:, :mod_columns]
    packed = mod_packed[:, mod_columns:].reshape(fsdp, -1, LANES)
    table_rows, temb = level_table.shape
    table_full = packed[:, :table_rows].reshape(fsdp * table_rows, temb)
    unpacked = []
    first = table_rows
    for vector in small:
        last = first + -(-vector.shape[0] // 128)
        rows = packed[:, first:last].reshape(fsdp, -1)[:, : vector.shape[0]]
        unpacked.append(rows.reshape(-1))
        first = last
    absorb_full, gain_attn, gain_mlp, up_bias_full, down_bias_full, mod_bias_full = unpacked
    model_width = tokens.shape[1]
    out_up = jnp.concatenate([out_weight, up_weight], axis=1)
    for _ in first_order:
        out_up, down_weight = advance((out_up, down_weight), qkv_chain)
    out_up_chain = Chain(gather_steps(out_up, fsdp, (first_order,)))
    down_chain = Chain(gather_steps(down_weight, fsdp, (second_order,)))
    qkv_full = qkv_chain.finish()
    seq_count = noise_level.shape[0]
    row_count = tokens.shape[0]
    length = row_count // seq_count
    levels = table_full.shape[0]
    level_picks = (jnp.arange(levels)[None, :] == noise_level[:, None]).astype(jnp.bfloat16)
    embedded = product(level_picks, table_full)
    cond_low = jax.nn.silu(embedded).astype(jnp.bfloat16)
    modulation = product(cond_low, mod_full) + mod_bias_full.astype(jnp.float32)
    pieces = jnp.split(modulation, 6, axis=1)
    shift_one, scale_one, gate_one, shift_two, scale_two, gate_two = [
        piece[:, None, :] for piece in pieces
    ]
    absorbed_rows = (absorbed > 0).reshape(seq_count, length, 1)
    start_rows = jnp.where(
        absorbed_rows,
        absorb_full.astype(jnp.float32)[None, None, :],
        tokens.astype(jnp.float32).reshape(seq_count, length, model_width),
    )
    gain_one = gain_attn.astype(jnp.float32)
    unit_one, inverse_one = normalize(start_rows)
    hidden_one = (
        (unit_one * gain_one * (1.0 + scale_one) + shift_one)
        .astype(jnp.bfloat16)
        .reshape(row_count, model_width)
    )
    projected = product(hidden_one, qkv_full)
    cosine, sine = rotary(length)
    group_sizes = [pair_count - pair_count // 3, pair_count // 3]
    starts = [0, group_sizes[0]]
    turned, mixed_parts, logs = ([], [], [])
    for start, pairs in zip(starts, group_sizes):
        if start == 0:
            projected = advance(projected, out_up_chain, down_chain)
        parts = attend(projected, cosine, sine, start, pairs, length)
        turned.append(parts[0])
        mixed_parts.append(parts[1])
        logs.append(parts[2])
    mixed_flat = jnp.concatenate(mixed_parts, axis=1)
    mixed_flat = advance(mixed_flat, out_up_chain, down_chain)
    out_up_full = out_up_chain.finish()
    out_full = out_up_full[:, :model_width]
    up_full = out_up_full[:, model_width:]
    attended = product(mixed_flat, out_full).reshape(seq_count, length, model_width)
    middle = start_rows + gate_one * attended
    gain_two = gain_mlp.astype(jnp.float32)
    unit_two, inverse_two = normalize(middle)
    hidden_two = (
        (unit_two * gain_two * (1.0 + scale_two) + shift_two)
        .astype(jnp.bfloat16)
        .reshape(row_count, model_width)
    )
    down_full = down_chain.finish()
    up_values = product(hidden_two, up_full) + up_bias_full.astype(jnp.float32)
    activated = jax.nn.gelu(up_values, approximate=True).astype(jnp.bfloat16)
    branch = (product(activated, down_full) + down_bias_full.astype(jnp.float32)).reshape(
        seq_count, length, model_width
    )
    block_out = (middle + gate_two * branch).reshape(row_count, model_width).astype(jnp.bfloat16)
    grad_out = cotangent.astype(jnp.float32).reshape(seq_count, length, model_width)
    d_gate_two = jnp.sum(grad_out * branch, axis=1)
    d_branch = (grad_out * gate_two).astype(jnp.bfloat16).reshape(row_count, model_width)
    g_down_bias = jnp.sum(d_branch.astype(jnp.float32), axis=0)
    down_sum = Chain(reduce_steps(product_left(activated, d_branch), fsdp, dp, second_order, True))
    d_up = (product_right(d_branch, down_full) * gelu_slope(up_values)).astype(jnp.bfloat16)
    d_up = advance(d_up, down_sum)
    g_up_bias = jnp.sum(d_up.astype(jnp.float32), axis=0)
    g_up = product_left(hidden_two, d_up).astype(jnp.bfloat16)
    d_up = advance(d_up, down_sum)
    d_hid_two = product_right(d_up, up_full).reshape(seq_count, length, model_width)
    d_shift_two = jnp.sum(d_hid_two, axis=1)
    d_scale_two = jnp.sum(d_hid_two * unit_two * gain_two, axis=1)
    g_gain_two = jnp.sum(d_hid_two * unit_two * (1.0 + scale_two), axis=(0, 1))
    d_middle = grad_out + norm_back(d_hid_two * gain_two * (1.0 + scale_two), unit_two, inverse_two)
    d_gate_one = jnp.sum(d_middle * attended, axis=1)
    d_attended = (d_middle * gate_one).astype(jnp.bfloat16).reshape(row_count, model_width)
    g_out = product_left(mixed_flat, d_attended).astype(jnp.bfloat16)
    out_up_sum = Chain(
        reduce_steps(jnp.concatenate([g_out, g_up], axis=1), fsdp, dp, first_order, True)
    )
    d_attended = advance(d_attended, down_sum)
    d_mixed = product_right(d_attended, out_full).astype(jnp.bfloat16)
    level_rows = jnp.broadcast_to(noise_level.astype(jnp.float32)[:, None], (seq_count, temb))
    early_sums = jnp.concatenate([g_gain_two, g_up_bias, g_down_bias])[None, :] / seq_count
    early = jnp.concatenate(
        [d_gate_one, d_shift_two, d_scale_two, d_gate_two, embedded, level_rows]
        + [jnp.broadcast_to(early_sums, (seq_count, early_sums.shape[1]))],
        axis=1,
    )
    early_chain = Chain(share_steps(early, fsdp, dp))
    open_sums = [down_sum, out_up_sum, early_chain]
    qkv_sums = []
    d_hid_one = 0.0
    for index, (start, pairs) in enumerate(zip(starts, group_sizes)):
        d_mixed = advance(d_mixed, *open_sums)
        d_group = attend_back(
            turned[index], d_mixed, logs[index], cosine, sine, start, pairs, length
        )
        part = qkv_full[:, start * 3 * LANES : (start + pairs) * 3 * LANES]
        d_hid_one = d_hid_one + product_right(d_group, part)
        g_group = product_left(hidden_one, d_group).astype(jnp.bfloat16)
        if start > 0:
            d_hid_one = advance(d_hid_one, *open_sums)
        order = second_order if start > 0 else first_order
        qkv_sums.append(Chain(reduce_steps(g_group, fsdp, dp, order, False)))
        open_sums.append(qkv_sums[-1])
    d_hid_one = d_hid_one.reshape(seq_count, length, model_width)
    d_shift_one = jnp.sum(d_hid_one, axis=1)
    d_scale_one = jnp.sum(d_hid_one * unit_one * gain_one, axis=1)
    g_gain_one = jnp.sum(d_hid_one * unit_one * (1.0 + scale_one), axis=(0, 1))
    d_start = d_middle + norm_back(d_hid_one * gain_one * (1.0 + scale_one), unit_one, inverse_one)
    tokens_grad = (
        jnp.where(absorbed_rows, 0.0, d_start).reshape(row_count, model_width).astype(jnp.bfloat16)
    )
    g_absorb = jnp.sum(jnp.where(absorbed_rows, d_start, 0.0), axis=(0, 1))
    width = model_width
    late_sums = jnp.concatenate([g_gain_one, g_absorb])[None, :] / seq_count
    late = jnp.concatenate(
        [d_shift_one, d_scale_one, jnp.broadcast_to(late_sums, (seq_count, late_sums.shape[1]))],
        axis=1,
    )
    late_all = Chain(share_steps(late, fsdp, dp)).finish()
    early_all = early_chain.finish()
    g_down = down_sum.finish()
    g_out_up = out_up_sum.finish()
    g_out = g_out_up[:, :width]
    g_up = g_out_up[:, width:]
    g_qkv = jnp.concatenate([chain.finish() for chain in qkv_sums], axis=1)
    g_qkv = g_qkv.reshape(-1, pair_count, 3, LANES).swapaxes(1, 2).reshape(qkv_weight.shape)
    d_mod = jnp.concatenate([late_all[:, : 2 * width], early_all[:, : 4 * width]], axis=1)
    embedded_all = early_all[:, 4 * width : 4 * width + temb].astype(jnp.float32)
    level_all = early_all[:, 4 * width + temb : 4 * width + temb + 1].astype(jnp.int32)
    early_totals = jnp.sum(early_all[:, 4 * width + 2 * temb :].astype(jnp.float32), axis=0)
    late_totals = jnp.sum(late_all[:, 2 * width :].astype(jnp.float32), axis=0)
    ff_width = up_bias_full.shape[0]
    g_gain_two = own_block(early_totals[:width], "fsdp", fsdp)
    g_up_bias = own_block(early_totals[width : width + ff_width], "fsdp", fsdp)
    g_down_bias = own_block(early_totals[width + ff_width :], "fsdp", fsdp)
    g_gain_one = own_block(late_totals[:width], "fsdp", fsdp)
    g_absorb = own_block(late_totals[width:], "fsdp", fsdp)
    cond_all = jax.nn.silu(embedded_all).astype(jnp.bfloat16)
    g_mod_bias = own_block(jnp.sum(d_mod.astype(jnp.float32), axis=0), "fsdp", fsdp)
    cond_own = lax.dynamic_slice_in_dim(
        cond_all, lax.axis_index("fsdp") * mod_weight.shape[0], mod_weight.shape[0], 1
    )
    g_mod = product_left(cond_own, d_mod)
    d_cond = product_right(d_mod, mod_full)
    sigmoid_of = jax.nn.sigmoid(embedded_all)
    d_embedded = d_cond * sigmoid_of * (1.0 + embedded_all * (1.0 - sigmoid_of))
    own_levels = lax.axis_index("fsdp") * table_rows + jnp.arange(table_rows)
    g_table = lax.dot_general(
        (level_all == own_levels[None, :]).astype(jnp.float32),
        d_embedded,
        (((0,), (0,)), ((), ())),
        precision=lax.Precision.HIGHEST,
    )
    owned_grads = (
        g_table,
        g_absorb,
        g_gain_one,
        g_qkv,
        g_out,
        g_gain_two,
        g_up,
        g_up_bias,
        g_down,
        g_down_bias,
        g_mod,
        g_mod_bias,
    )
    return (block_out, tokens_grad) + owned_grads


def solution(mesh):
    return jax.shard_map(
        body,
        mesh=mesh,
        in_specs=(
            P(("fsdp", "dp"), None),
            P(("fsdp", "dp")),
            P(("fsdp", "dp")),
            P(("fsdp", "dp"), None),
            P("fsdp", None),
            P("fsdp"),
            P("fsdp"),
            P("fsdp", None),
            P("fsdp", None),
            P("fsdp"),
            P("fsdp", None),
            P("fsdp"),
            P("fsdp", None),
            P("fsdp"),
            P("fsdp", None),
            P("fsdp"),
        ),
        out_specs=(
            P(("fsdp", "dp"), None),
            P(("fsdp", "dp"), None),
            P("fsdp", None),
            P("fsdp"),
            P("fsdp"),
            P("fsdp", None),
            P("fsdp", None),
            P("fsdp"),
            P("fsdp", None),
            P("fsdp"),
            P("fsdp", None),
            P("fsdp"),
            P("fsdp", None),
            P("fsdp"),
        ),
        check_vma=False,
    )
```
